32 devices in a mesh: dp: 2 (over core), dom: 16 (over z, y, x).
Axes of the slice: x: 2, y: 2, z: 4, core: 2. Of those that a mesh axis runs over, the one named last changes fastest.
Arguments:
- features: bfloat16 [2, 6144, 512], P('dp', 'dom'), may hold values from -12 to 12
- tile_mask: int32 [2, 48, 18], P('dp', 'dom'), may hold values from 0 to 1, as said below
- cotangent: bfloat16 [2, 6144, 512], P('dp', 'dom'), may hold values from -6 to 6
- w_query: bfloat16 [512, 512], replicated, may hold values from -1 to 1
- w_key: bfloat16 [512, 512], replicated, may hold values from -1 to 1
- w_value: bfloat16 [512, 512], replicated, may hold values from -0.25 to 0.25
- w_out: bfloat16 [512, 512], replicated, may hold values from -0.25 to 0.25
Outputs:
- attended: bfloat16 [2, 6144, 512], P('dp', 'dom')
- grad_features: bfloat16 [2, 6144, 512], P('dp', 'dom')
- grad_query: float32 [512, 512], replicated
- grad_key: float32 [512, 512], replicated
- grad_value: float32 [512, 512], replicated
- grad_out: float32 [512, 512], replicated
The draws below stay inside these ranges and needn't reach their ends.
Inputs may be any that keep to these rules, and one draw needn't show every extreme that they name: `tile_mask`: 0 or 1; the share of ones differs between tile groups, from about a quarter to all.
All inputs are finite; a program needn't handle non-finite values.
Results may differ from the reference program's by a relative error of at most 0.023.
Values may be sent and summed in bfloat16 or wider, within the bound.
No kernel may reach another device: no remote copies, remote signals or barrier semaphores. Data moves between devices by JAX's collectives and lax.ppermute only.
A program may use at most 128 MiB of HBM per device.

```python
import jax
import jax.numpy as jnp
from jax import lax

HEADS = 8
HEAD_DIM = 64
D = 512
TILE = 128
TILE_DEV = 3
NB = 3
CANDT = 18
QT = 48
NODES = 6144
WINDOWS = 2
N_DOM = 16


def draw_tile_mask(key, part):
    groups = QT // TILE_DEV
    level_key, bit_key = jax.random.split(jax.random.fold_in(key, 11))
    levels = jax.random.randint(level_key, (WINDOWS, groups, 1, 1), 1, 5)
    draws = jax.random.randint(bit_key, (WINDOWS, groups, TILE_DEV, CANDT), 0, 4)
    return (draws < levels).astype(jnp.int32).reshape(WINDOWS, QT, CANDT)


def weight_pair(key):
    primary_key, secondary_key = jax.random.split(jax.random.fold_in(key, 31))
    primary = jnp.clip(jax.random.normal(primary_key, (D, D), jnp.float32), -6.0, 6.0) * D ** (-0.5)
    secondary = jnp.clip(jax.random.normal(secondary_key, (D, D), jnp.float32), -6.0, 6.0) * D ** (-0.5)
    return (primary, secondary)


def draw_w_query(key, part):
    primary, secondary = weight_pair(key)
    return primary.astype(jnp.bfloat16)


def draw_w_key(key, part):
    primary, secondary = weight_pair(key)
    return secondary.astype(jnp.bfloat16)


def draw_features(key, part):
    pieces = jax.random.split(jax.random.fold_in(key, 23), 7)
    drawn = jnp.clip(jax.random.normal(pieces[6], (WINDOWS, NODES, D), jnp.float32), -6.0, 6.0)
    return drawn.astype(jnp.bfloat16)


def block_scale(rng, dims, cuts, least, top_value):
    level = 1.0
    for dim, blocks in cuts:
        heights = jax.random.uniform(jax.random.fold_in(jax.random.fold_in(rng, 6), dim), (blocks,), jnp.float32, least / len(cuts), top_value / len(cuts))
        level = level * jnp.repeat(jnp.exp(heights), dims[dim] // blocks).reshape((-1,) + (1,) * (len(dims) - 1 - dim))
    return level


def centred(rng, dims, scale, most, cuts=(), kind=jnp.bfloat16):
    values = scale * jax.random.normal(rng, dims, jnp.float32)
    if cuts:
        values = values * block_scale(rng, dims, cuts, -0.22, 0.18)
    return jnp.clip(values, -most, most).astype(kind)


def setup_inputs(seed: int = 0) -> dict:
    key_list = jax.random.split(jax.random.key(seed), 8)
    return {
        "features": draw_features(jax.random.fold_in(key_list[7], 71), 0),
        "tile_mask": draw_tile_mask(jax.random.fold_in(key_list[7], 71), 0),
        "cotangent": centred(key_list[2], (WINDOWS, NODES, D), 1.0, 6.0, ((0, 2), (1, 16))),
        "w_query": draw_w_query(jax.random.fold_in(key_list[7], 71), 0),
        "w_key": draw_w_key(jax.random.fold_in(key_list[7], 71), 0),
        "w_value": centred(key_list[5], (D, D), D ** -0.5, 0.25),
        "w_out": centred(key_list[6], (D, D), D ** -0.5, 0.25),
    }


def candidates(device):
    levels = N_DOM.bit_length() - 1
    found = [device, (device - 1) % N_DOM, (device + 1) % N_DOM]
    for bit_step in range(NB):
        found.append(jnp.bitwise_xor(device, jnp.int32(2 ** (levels - 1 - bit_step))))
    return found


def live_table(mask_rows):
    own_tile = jnp.arange(CANDT)[None, :] == jnp.arange(TILE_DEV)[:, None]
    return (mask_rows == 1) | own_tile


def attend(q_rows, cand_kv, live_tiles):
    block_rows = q_rows.shape[0]
    key_count = cand_kv.shape[0]
    head_q = q_rows.reshape(block_rows, HEADS, HEAD_DIM).astype(jnp.float32)
    head_k = cand_kv[:, :D].reshape(key_count, HEADS, HEAD_DIM).astype(jnp.float32)
    head_v = cand_kv[:, D:].reshape(key_count, HEADS, HEAD_DIM).astype(jnp.float32)
    scores = jnp.einsum("rhd,chd->hrc", head_q, head_k) * HEAD_DIM ** -0.5
    masking = jnp.where(live_tiles, 0.0, -1e30).astype(jnp.float32)
    scores = scores.reshape(HEADS, TILE_DEV, TILE, CANDT, TILE) + masking[None, :, None, :, None]
    scores = scores.reshape(HEADS, block_rows, key_count)
    row_max = jnp.max(scores, axis=2, keepdims=True)
    exp_vals = jnp.exp(scores - row_max)
    prob_f32 = exp_vals / jnp.sum(exp_vals, axis=2, keepdims=True)
    prob_bf = lax.optimization_barrier(prob_f32.astype(jnp.bfloat16)).astype(jnp.float32)
    out_rows = jnp.einsum("hrc,chd->rhd", prob_bf, head_v).reshape(block_rows, D).astype(jnp.bfloat16)
    return head_q, head_k, head_v, prob_f32, prob_bf, out_rows


def attend_back(head_q, head_k, head_v, prob_f32, prob_bf, out_rows, grad_o):
    block_rows = head_q.shape[0]
    key_count = head_k.shape[0]
    g_heads = grad_o.reshape(block_rows, HEADS, HEAD_DIM).astype(jnp.float32)
    grad_prob = jnp.einsum("rhd,chd->hrc", g_heads, head_v)
    row_delta = jnp.einsum("rhd,rhd->hr", g_heads, out_rows.reshape(block_rows, HEADS, HEAD_DIM).astype(jnp.float32))
    grad_score = (prob_f32 * (grad_prob - row_delta[:, :, None]) * HEAD_DIM ** -0.5).astype(jnp.bfloat16)
    score_f32 = lax.optimization_barrier(grad_score).astype(jnp.float32)
    grad_q = jnp.einsum("hrc,chd->rhd", score_f32, head_k).reshape(block_rows, D)
    grad_k = jnp.einsum("hrc,rhd->chd", score_f32, head_q).reshape(key_count, D)
    grad_v = jnp.einsum("hrc,rhd->chd", prob_bf, g_heads).reshape(key_count, D)
    return grad_q, jnp.concatenate([grad_k, grad_v], 1)


def window(node_rows, mask_rows, cotangent, w_query, w_both, w_out):
    block_rows = TILE_DEV * TILE
    q_all = jnp.dot(node_rows, w_query, preferred_element_type=jnp.float32).astype(jnp.bfloat16)
    kv_all = jnp.dot(node_rows, w_both, preferred_element_type=jnp.float32).astype(jnp.bfloat16)

    def per_device(grad_acc, device):
        row_start = device * block_rows
        q_rows = lax.dynamic_slice_in_dim(q_all, row_start, block_rows, 0)
        sources = candidates(device)
        cand_kv = jnp.concatenate([lax.dynamic_slice_in_dim(kv_all, (source * block_rows).astype(jnp.int32), block_rows, 0) for source in sources], 0)
        live_tiles = live_table(lax.dynamic_slice_in_dim(mask_rows, (device * TILE_DEV).astype(jnp.int32), TILE_DEV, 0))
        head_q, head_k, head_v, prob_f32, prob_bf, out_rows = attend(q_rows, cand_kv, live_tiles)
        y_rows = jnp.dot(out_rows, w_out, preferred_element_type=jnp.float32).astype(jnp.bfloat16)
        cot_rows = lax.dynamic_slice_in_dim(cotangent, row_start, block_rows, 0)
        grad_o = jnp.dot(cot_rows, w_out.T, preferred_element_type=jnp.float32).astype(jnp.bfloat16)
        grad_q, grad_kv = attend_back(head_q, head_k, head_v, prob_f32, prob_bf, out_rows, grad_o)
        for slot_index, source in enumerate(sources):
            src_start = (source * block_rows).astype(jnp.int32)
            current = lax.dynamic_slice_in_dim(grad_acc, src_start, block_rows, 0)
            piece = grad_kv[slot_index * block_rows:(slot_index + 1) * block_rows]
            grad_acc = lax.dynamic_update_slice_in_dim(grad_acc, current + piece, src_start, 0)
        return grad_acc, (y_rows, out_rows, grad_q)

    grad_acc, stacked = lax.scan(per_device, jnp.zeros((NODES, 2 * D), jnp.float32), jnp.arange(N_DOM, dtype=jnp.int32))
    y_all = stacked[0].reshape(NODES, D)
    o_all = stacked[1].reshape(NODES, D)
    grad_q_all = stacked[2].reshape(NODES, D)
    highest = lax.Precision.HIGHEST
    grad_x = jnp.dot(grad_q_all, w_query.T.astype(jnp.float32), precision=highest)
    grad_x = (grad_x + jnp.dot(grad_acc, w_both.T.astype(jnp.float32), precision=highest)).astype(jnp.bfloat16)
    rows_f32 = node_rows.astype(jnp.float32)
    g_query = jnp.dot(rows_f32.T, grad_q_all, precision=highest)
    g_both = jnp.dot(rows_f32.T, grad_acc, precision=highest)
    g_out = jnp.dot(o_all.T, cotangent, preferred_element_type=jnp.float32)
    return y_all, grad_x, g_query, g_both, g_out


def reference(features, tile_mask, cotangent, w_query, w_key, w_value, w_out):
    w_both = jnp.concatenate([w_key, w_value], 1)
    y_list = []
    gx_list = []
    g_query = jnp.zeros((D, D), jnp.float32)
    g_both = jnp.zeros((D, 2 * D), jnp.float32)
    g_out = jnp.zeros((D, D), jnp.float32)
    for window_index in range(WINDOWS):
        y_all, grad_x, gq_part, gb_part, go_part = window(features[window_index], tile_mask[window_index], cotangent[window_index], w_query, w_both, w_out)
        y_list.append(y_all)
        gx_list.append(grad_x)
        g_query = g_query + gq_part
        g_both = g_both + gb_part
        g_out = g_out + go_part
    return (jnp.stack(y_list), jnp.stack(gx_list), g_query, g_both[:, :D], g_both[:, D:], g_out)
```

```python
import jax
import jax.numpy as jnp
from jax import lax
from jax.experimental import pallas as pl
from jax.experimental.pallas import tpu as pltpu
from jax.sharding import PartitionSpec as P

HEAD_DIM = 64
TILE = 128
NB = 3
LANES = 128
NT = (((1,), (1,)), ((), ()))
NN = (((1,), (0,)), ((), ()))
TN = (((0,), (0,)), ((), ()))
F32 = jnp.float32
BF = jnp.bfloat16


def exchanged(value, axis, mask):
    pairs = [(source, source ^ mask) for source in range(lax.axis_size(axis))]
    return lax.ppermute(value, axis, pairs)


def shifted(value, axis, step):
    count = lax.axis_size(axis)
    return lax.ppermute(value, axis, [(i, (i + step) % count) for i in range(count)])


def attention_kernel(
    q_ref, k_ref, v_ref, go_ref, bias_ref, o_ref, gq_ref, gk_ref, gv_ref,
    k_aug, v_aug, exp_all, score_all, q_all, go_all,
):
    rows = q_ref.shape[0]
    keys = k_ref.shape[0]
    lane = lax.broadcasted_iota(jnp.int32, (rows, LANES), 1)
    row = lax.broadcasted_iota(jnp.int32, (rows, LANES), 0)
    k_aug[:, :LANES] = k_ref[...]
    k_aug[:, LANES:] = bias_ref[...]
    v_aug[:, :LANES] = v_ref[...]
    v_aug[:, LANES:] = jnp.ones((keys, LANES), BF)
    one_hot = (row // TILE == lane).astype(F32).astype(BF)
    factor = HEAD_DIM**-0.5
    q_pair = q_ref[...].astype(F32) * factor
    go_pair = go_ref[...].astype(F32)
    outs = []
    grads = []
    for head in range(2):
        mine = (lane < HEAD_DIM) if head == 0 else (lane >= HEAD_DIM)
        span = pl.ds(head * rows, rows)
        q_head = jnp.where(mine, q_pair, 0.0).astype(BF)
        q_all[span, :] = q_head
        scores = lax.dot_general(
            jnp.concatenate([q_head, one_hot], 1), k_aug[...], NT, preferred_element_type=F32
        )
        row_max = jnp.max(scores, axis=1, keepdims=True)
        exp_vals = jnp.exp(scores - row_max).astype(BF)
        exp_all[span, :] = exp_vals
        summed = lax.dot_general(exp_vals, v_aug[...], NN, preferred_element_type=F32)
        inverse = 1.0 / summed[:, LANES:]
        out = (summed[:, :LANES] * inverse).astype(BF)
        outs.append(out)
        go_head = jnp.where(mine, go_pair * inverse, 0.0).astype(BF)
        go_all[span, :] = go_head
        delta = jnp.sum(go_head.astype(F32) * out.astype(F32), axis=1, keepdims=True)
        high = delta.astype(BF).astype(F32)
        low = delta - high
        less = jnp.where(lane == 0, -high, jnp.where(lane == 1, -low, 0.0)).astype(BF)
        grad_prob = lax.dot_general(
            jnp.concatenate([go_head, less], 1), v_aug[...], NT, preferred_element_type=F32
        )
        grad_score = grad_prob.astype(BF) * exp_vals
        score_all[span, :] = grad_score
        grads.append(
            lax.dot_general(grad_score, k_aug[:, :LANES], NN, preferred_element_type=F32) * factor
        )
    first = lane < HEAD_DIM
    o_ref[...] = jnp.where(first, outs[0].astype(F32), outs[1].astype(F32)).astype(BF)
    gq_ref[...] = jnp.where(first, grads[0], grads[1]).astype(BF)
    gv_ref[...] = lax.dot_general(
        go_all[...].T, exp_all[...], NN, preferred_element_type=F32
    ).astype(BF)
    gk_ref[...] = lax.dot_general(
        q_all[...].T, score_all[...], NN, preferred_element_type=F32
    ).astype(BF)


def attention(q, k, v, go, bias):
    rows, width = q.shape
    keys = k.shape[0]
    by_rows = pl.BlockSpec((rows, LANES), lambda pair: (0, pair))
    by_keys = pl.BlockSpec((keys, LANES), lambda pair: (0, pair))
    turned = pl.BlockSpec((LANES, keys), lambda pair: (pair, 0))
    return pl.pallas_call(
        attention_kernel,
        grid=(width // LANES,),
        in_specs=[
            by_rows, by_keys, by_keys, by_rows, pl.BlockSpec((keys, LANES), lambda pair: (0, 0)),
        ],
        out_specs=[by_rows, by_rows, turned, turned],
        out_shape=[
            jax.ShapeDtypeStruct((rows, width), BF),
            jax.ShapeDtypeStruct((rows, width), BF),
            jax.ShapeDtypeStruct((width, keys), BF),
            jax.ShapeDtypeStruct((width, keys), BF),
        ],
        scratch_shapes=[
            pltpu.VMEM((keys, 2 * LANES), BF),
            pltpu.VMEM((keys, 2 * LANES), BF),
            pltpu.VMEM((2 * rows, keys), BF),
            pltpu.VMEM((2 * rows, keys), BF),
            pltpu.VMEM((2 * rows, LANES), BF),
            pltpu.VMEM((2 * rows, LANES), BF),
        ],
        compiler_params=pltpu.CompilerParams(vmem_limit_bytes=60 * 1024 * 1024),
        name="attention",
    )(q, k, v, go, bias)


def sum_stages():
    stages = [("dp", (1,), 0)]
    bits = lax.axis_size("dom").bit_length() - 1
    bit = 0
    while bit < bits:
        width = min(2, bits - bit)
        stages.append(("dom", tuple(m << bit for m in range(1, 1 << width)), bit))
        bit += width
    return stages


def chunk_of(value, index, count):
    size = value.shape[0] // count
    return lax.dynamic_slice_in_dim(value, index * size, size, 0)


def summed_over_devices(value):
    stages = sum_stages()
    for axis, masks, bit in stages:
        count = len(masks) + 1
        mine = (lax.axis_index(axis) >> bit) % count
        total = chunk_of(value, mine, count).astype(F32)
        for mask in masks:
            sent = chunk_of(value, mine ^ (mask >> bit), count)
            total = total + exchanged(sent, axis, mask).astype(F32)
        value = total.astype(BF)
    for axis, masks, bit in reversed(stages):
        count = len(masks) + 1
        mine = (lax.axis_index(axis) >> bit) % count
        size = value.shape[0]
        whole = jnp.zeros((count * size,) + value.shape[1:], BF)
        whole = lax.dynamic_update_slice_in_dim(whole, value, mine * size, 0)
        for mask in masks:
            got = exchanged(value, axis, mask)
            whole = lax.dynamic_update_slice_in_dim(whole, got, (mine ^ (mask >> bit)) * size, 0)
        value = whole
    return value


def per_device(features, tile_mask, cotangent, w_query, w_key, w_value, w_out):
    x = features[0]
    rows, width = x.shape
    cot = cotangent[0]
    levels = lax.axis_size("dom").bit_length() - 1
    steps = [1 << (levels - 1 - j) for j in range(NB)]
    far = [exchanged(x, "dom", step) for step in steps]
    below = shifted(x, "dom", 1)
    above = shifted(x, "dom", -1)
    w_both = jnp.concatenate([w_key, w_value], 1)
    q = jnp.dot(x, w_query, preferred_element_type=F32).astype(BF)
    go = lax.dot_general(cot, w_out, NT, preferred_element_type=F32).astype(BF)
    tiles, cands = tile_mask.shape[1:]
    own = jnp.arange(cands)[None, :] == jnp.arange(tiles)[:, None]
    live = (tile_mask[0] == 1) | own
    bias = jnp.pad(jnp.where(live, 0.0, -1e30).T, ((0, 0), (0, LANES - tiles)))
    bias = jnp.repeat(bias.astype(BF), TILE, axis=0)
    cand = jnp.concatenate([x, below, above] + far, 0)
    k = jnp.dot(cand, w_key, preferred_element_type=F32).astype(BF)
    v = jnp.dot(cand, w_value, preferred_element_type=F32).astype(BF)
    o, gq, gk, gv = attention(q, k, v, go, bias)
    attended = jnp.dot(o, w_out, preferred_element_type=F32).astype(BF)
    contrib = lax.dot_general(gk, w_key, (((0,), (1,)), ((), ())), preferred_element_type=F32)
    contrib = contrib + lax.dot_general(
        gv, w_value, (((0,), (1,)), ((), ())), preferred_element_type=F32
    )
    parts = contrib.reshape(3 + NB, rows, width)
    sent = parts.astype(BF)
    back = [exchanged(sent[3 + j], "dom", steps[j]) for j in range(NB)]
    back.append(shifted(sent[1], "dom", -1))
    back.append(shifted(sent[2], "dom", 1))
    grad_x = parts[0] + lax.dot_general(gq, w_query, NT, preferred_element_type=F32)
    g_query = lax.dot_general(x, gq, TN, preferred_element_type=F32)
    g_key = lax.dot_general(cand, gk, (((0,), (1,)), ((), ())), preferred_element_type=F32)
    g_value = lax.dot_general(cand, gv, (((0,), (1,)), ((), ())), preferred_element_type=F32)
    g_out = lax.dot_general(o, cot, TN, preferred_element_type=F32)
    grads = jnp.concatenate([g.astype(BF) for g in (g_query, g_key, g_value, g_out)], 0)
    grads = summed_over_devices(grads).astype(F32)
    for part in back:
        grad_x = grad_x + part.astype(F32)
    g_query, g_key, g_value, g_out = jnp.split(grads, 4, 0)
    return (attended[None], grad_x.astype(BF)[None], g_query, g_key, g_value, g_out)


def solution(mesh):
    split = P("dp", "dom", None)
    return jax.shard_map(
        per_device,
        mesh=mesh,
        in_specs=(split, split, split, P(), P(), P(), P()),
        out_specs=(split, split, P(), P(), P(), P()),
        check_vma=False,
    )
```
